32 devices in a mesh: ctx: 4 (over z), node: 4 (over y, core), local: 2 (over x).
Axes of the slice: x: 2, y: 2, z: 4, core: 2. Of those that a mesh axis runs over, the one named last changes fastest.
Arguments:
- tokens: bfloat16 [1024, 3584], P(('node', 'local'), 'ctx'), may hold values from -6 to 6
- expert_ids: int32 [1024, 4], P(('node', 'local')), may hold values from 0 to 7, as said below
- route_scores: float32 [1024, 4], P(('node', 'local')), may hold values from 0.05 to 1
- w_gate: bfloat16 [8, 3584, 2048], P(('node', 'local'), None, 'ctx'), may hold values from -0.09375 to 0.09375
- w_up: bfloat16 [8, 3584, 2048], P(('node', 'local'), None, 'ctx'), may hold values from -0.09375 to 0.09375
- w_down: bfloat16 [8, 2048, 3584], P(('node', 'local'), None, 'ctx'), may hold values from -0.125 to 0.125
- shared_gate: bfloat16 [3584, 2048], P(None, 'ctx'), may hold values from -0.09375 to 0.09375
- shared_up: bfloat16 [3584, 2048], P(None, 'ctx'), may hold values from -0.09375 to 0.09375
- shared_down: bfloat16 [2048, 3584], P(None, 'ctx'), may hold values from -0.125 to 0.125
Outputs:
- mixed: bfloat16 [1024, 3584], P(('node', 'local'), 'ctx')
The draws below stay inside these ranges and needn't reach their ends.
Inputs may be any that keep to these rules, and one draw needn't show every extreme that they name: `expert_ids`: each row names 4 different experts: two in each of two different node groups, where expert e lies in group e // 2. In each aligned block of 128 rows (the rows of one index of node+local) no group is named by more than 80 rows and no expert more than 80 times; one group, the same in every block, is named by exactly 80 rows in every block, and one of its experts, the same in every block, exactly 80 times.
All inputs are finite; a program needn't handle non-finite values.
Results may differ from the reference program's by a relative error of at most 0.0064.
Values may be sent and summed in bfloat16 or wider, within the bound.
A program may use at most 64 MiB of HBM per device.

```python
import math
import jax
import jax.numpy as jnp
from jax import lax

D = 3584
FF = 2048
TOK_DEV = 128
TOPK = 4
GROUPS = 4
GROUP_EXPERTS = 2
EXPERTS = 8
GCAP = 80
SLOTS = 640
TOKENS = 1024
N_NODE = 4
N_LOCAL = 2


def draw_expert_ids(key, part):
    picks = 2 * TOK_DEV
    group_slots = GROUPS * GCAP
    blocks = N_NODE * N_LOCAL
    favored_group = jax.random.randint(jax.random.fold_in(key, 7), (), 0, GROUPS)
    favored_local = jax.random.randint(jax.random.fold_in(key, 8), (), 0, GROUP_EXPERTS)
    owners = jnp.arange(group_slots, dtype=jnp.int32) // GCAP
    group_range = jnp.arange(GROUPS, dtype=jnp.int32)
    local_range = jnp.arange(GROUP_EXPERTS, dtype=jnp.int32)

    def one_block(block_key):
        first_key, second_key, third_key, fourth_key = jax.random.split(block_key, 4)
        priority = jax.random.permutation(first_key, group_slots).astype(jnp.int32)
        priority = jnp.where(owners == favored_group, priority - group_slots, priority)
        ordering = jnp.argsort(priority, stable=True)
        chosen = jnp.sort(ordering[:picks])
        group_list = (chosen // GCAP).astype(jnp.int32)
        table = group_list.reshape(2, TOK_DEV).T
        table = table[jax.random.permutation(second_key, TOK_DEV)]
        joined = jnp.any(table[:, :, None] == group_range[None, None, :], axis=1).astype(jnp.int32)
        group_rank = jnp.cumsum(joined, axis=0) - joined
        rank_pick = jnp.take_along_axis(group_rank, table, axis=1)
        perm_keys = jax.random.split(third_key, GROUPS)
        perms = jax.vmap(lambda one_key: jax.random.permutation(one_key, GROUP_EXPERTS))(perm_keys).astype(jnp.int32)
        position = jnp.argsort(perms, axis=1).astype(jnp.int32)
        forced = (group_range[:, None] == favored_group) & (local_range[None, :] == favored_local)
        position = jnp.where(forced, -1, position)
        perm_table = jnp.argsort(position, axis=1, stable=True).astype(jnp.int32)
        first_pos = 2 * rank_pick % GROUP_EXPERTS
        second_pos = (2 * rank_pick + 1) % GROUP_EXPERTS
        first_local = perm_table[table, first_pos]
        second_local = perm_table[table, second_pos]
        first_ids = table * GROUP_EXPERTS + first_local
        second_ids = table * GROUP_EXPERTS + second_local
        ids = jnp.stack([first_ids[:, 0], second_ids[:, 0], first_ids[:, 1], second_ids[:, 1]], axis=1)
        scores = jax.random.randint(fourth_key, (TOK_DEV, TOPK), 0, 1 << 20) * TOPK + jnp.arange(TOPK, dtype=jnp.int32)[None, :]
        order = jnp.argsort(scores, axis=1)
        return jnp.take_along_axis(ids, order, axis=1).astype(jnp.int32)
    block_keys = jax.random.split(jax.random.fold_in(key, 11), blocks)
    result = jax.vmap(one_block)(block_keys)
    return result.reshape(blocks * TOK_DEV, TOPK).astype(jnp.int32)


def block_levels(stream_key, extent, cuts, smallest, largest):
    def one(dim, blocks):
        steps = jax.random.uniform(jax.random.fold_in(jax.random.fold_in(stream_key, 6), dim), (blocks,), jnp.float32, smallest / len(cuts), largest / len(cuts))
        return jnp.repeat(jnp.exp(steps), extent[dim] // blocks).reshape((-1,) + (1,) * (len(extent) - dim - 1))

    level = one(*cuts[0])
    for cut in cuts[1:]:
        level = level * one(*cut)
    return level


def bell_draw(key, shape, width, most, pieces=(), held_as=jnp.bfloat16):
    entries = jax.random.normal(key, shape, jnp.float32) * width
    if len(pieces) > 0:
        entries = block_levels(key, shape, pieces, -0.22, 0.18) * entries
    return jnp.clip(entries, min=-most, max=most).astype(held_as)


def setup_inputs(seed: int = 0) -> dict:
    key_list = jax.random.split(jax.random.key(seed), 10)
    return {
        "tokens": bell_draw(key_list[0], (TOKENS, D), 1.0, 6.0, ((0, 8), (1, 4))),
        "expert_ids": draw_expert_ids(jax.random.fold_in(key_list[9], 71), 0),
        "route_scores": jnp.clip(jnp.exp(math.log(1.0) - 2.9957323 * jax.random.uniform(key_list[2], (TOKENS, TOPK), jnp.float32) ** block_levels(key_list[2], (TOKENS, TOPK), ((0, 8),), -0.2, 0.2)), 0.05, 1.0),
        "w_gate": bell_draw(key_list[3], (EXPERTS, D, FF), D ** -0.5, 0.09375, ((0, 8), (2, 4))),
        "w_up": bell_draw(key_list[4], (EXPERTS, D, FF), D ** -0.5, 0.09375, ((0, 8), (2, 4))),
        "w_down": bell_draw(key_list[5], (EXPERTS, FF, D), FF ** -0.5, 0.125, ((0, 8), (2, 4))),
        "shared_gate": bell_draw(key_list[6], (D, FF), D ** -0.5, 0.09375, ((1, 4),)),
        "shared_up": bell_draw(key_list[7], (D, FF), D ** -0.5, 0.09375, ((1, 4),)),
        "shared_down": bell_draw(key_list[8], (FF, D), FF ** -0.5, 0.125, ((1, 4),)),
    }


route_scale = 2.5


def expert_pass(inputs, gate_matrix, up_matrix, down_matrix):
    gate_value = jnp.dot(inputs, gate_matrix, preferred_element_type=jnp.float32)
    up_value = jnp.dot(inputs, up_matrix, preferred_element_type=jnp.float32)
    hidden = (jax.nn.silu(gate_value) * up_value).astype(jnp.bfloat16)
    return jnp.dot(hidden, down_matrix, preferred_element_type=jnp.float32)


def reference(tokens, expert_ids, route_scores, w_gate, w_up, w_down, shared_gate, shared_up, shared_down):
    scaled = route_scale * route_scores / jnp.sum(route_scores, axis=1, keepdims=True)
    gate_weights = lax.optimization_barrier(scaled.astype(jnp.bfloat16)).astype(jnp.float32)
    shared_out = expert_pass(tokens, shared_gate, shared_up, shared_down)

    def one_expert(index):
        chosen = expert_ids == index
        member = jnp.any(chosen, axis=1)
        weight_column = jnp.sum(jnp.where(chosen, gate_weights, 0.0), axis=1)
        positions = jnp.nonzero(member, size=SLOTS, fill_value=0)[0].astype(jnp.int32)
        valid = jnp.arange(SLOTS, dtype=jnp.int32) < jnp.sum(member.astype(jnp.int32))
        outputs = expert_pass(tokens[positions], w_gate[index], w_up[index], w_down[index]).astype(jnp.bfloat16)
        outputs = lax.optimization_barrier(outputs).astype(jnp.float32)
        scale_column = jnp.where(valid, weight_column[positions], 0.0)
        return positions, outputs * scale_column[:, None]

    positions, contribs = lax.map(one_expert, jnp.arange(EXPERTS, dtype=jnp.int32))
    positions = positions.reshape(GROUPS, GROUP_EXPERTS * SLOTS)
    contribs = contribs.reshape(GROUPS, GROUP_EXPERTS * SLOTS, D)

    def add_group(group, total):
        routed = jnp.zeros((TOKENS, D), jnp.float32).at[positions[group]].add(contribs[group])
        rounded = lax.optimization_barrier(routed.astype(jnp.bfloat16)).astype(jnp.float32)
        return total + rounded

    mixed = lax.fori_loop(0, GROUPS, add_group, shared_out.astype(jnp.float32))
    return mixed.astype(jnp.bfloat16)
```

```python
import jax
import jax.numpy as jnp
from jax import lax
from jax.experimental import pallas as pl
from jax.experimental.pallas import tpu as pltpu
from jax.sharding import PartitionSpec as P

route_scale = 2.5
MESH = pl.DeviceIdType.MESH
VMEM_BYTES = 64000 * 1024


def matmul(left_side, right_side):
    return jnp.dot(left_side, right_side, preferred_element_type=jnp.float32)


def exchange(
    tokens, expert_ids, route_scores, w_gate, w_up, w_down, shared_gate, shared_up, shared_down
):
    tok_count = tokens.shape[0]
    feat_local = tokens.shape[1]
    top_count = expert_ids.shape[1]
    group_count = lax.axis_size("node")
    member_count = lax.axis_size("local")
    expert_count = group_count * member_count
    group_cap = (10 * tok_count + 4 * group_count - 1) // (4 * group_count)
    capacity = (2 * group_cap + member_count - 1) // member_count
    slot_total = expert_count * capacity
    gate_local = w_gate[0]
    up_local = w_up[0]
    down_local = w_down[0]
    out_width = down_local.shape[1]
    scaled = route_scale * route_scores / jnp.sum(route_scores, axis=1, keepdims=True)
    gate_weights = lax.optimization_barrier(scaled.astype(jnp.bfloat16)).astype(jnp.float32)
    group_range = jnp.arange(group_count, dtype=jnp.int32)
    group_onehot = (expert_ids // member_count)[:, :, None] == group_range[None, None, :]
    flat_ids = expert_ids.reshape(-1)
    pair_count = flat_ids.shape[0]
    onehot = (flat_ids[:, None] == jnp.arange(expert_count, dtype=jnp.int32)[None, :]).astype(
        jnp.int32
    )
    earlier = jnp.cumsum(onehot, axis=0) - onehot
    ranking = jnp.sum(earlier * onehot, axis=1)
    pair_slot = flat_ids * capacity + ranking
    pair_token = jnp.arange(pair_count, dtype=jnp.int32) // top_count
    matches = pair_slot[None, :] == jnp.arange(slot_total, dtype=jnp.int32)[:, None]
    slot_token = jnp.where(
        jnp.any(matches, axis=1),
        jnp.sum(jnp.where(matches, pair_token[None, :], 0), axis=1),
        tok_count,
    )
    padded_tokens = jnp.concatenate([tokens, jnp.zeros((1, feat_local), tokens.dtype)], axis=0)
    send_rows = padded_tokens[slot_token].reshape(group_count, member_count, capacity * feat_local)
    arrived = lax.all_to_all(
        lax.all_to_all(send_rows, "node", split_axis=0, concat_axis=0, tiled=True),
        "local",
        split_axis=1,
        concat_axis=1,
        tiled=True,
    )
    routed_rows = arrived.reshape(slot_total, feat_local)
    stacked = jnp.concatenate([routed_rows, tokens], axis=0)
    segment = lax.all_gather(stacked, "ctx", axis=1, tiled=True)
    routed_part = segment[:slot_total]
    shared_part = segment[slot_total:]
    gate_routed = matmul(routed_part, gate_local)
    up_routed = matmul(routed_part, up_local)
    gate_shared = matmul(shared_part, shared_gate)
    up_shared = matmul(shared_part, shared_up)
    routed_hidden = (jax.nn.silu(gate_routed) * up_routed).astype(jnp.bfloat16)
    shared_hidden = (jax.nn.silu(gate_shared) * up_shared).astype(jnp.bfloat16)
    hidden_stack = jnp.concatenate([routed_hidden, shared_hidden], axis=0)
    segment = lax.all_gather(hidden_stack, "ctx", axis=1, tiled=True)
    routed_out = matmul(segment[:slot_total], down_local)
    shared_out = matmul(segment[slot_total:], shared_down)
    routed_bf = routed_out.astype(jnp.bfloat16)
    sendback = routed_bf.reshape(group_count, member_count, capacity * out_width)
    returned = lax.all_to_all(
        lax.all_to_all(sendback, "node", split_axis=0, concat_axis=0, tiled=True),
        "local",
        split_axis=1,
        concat_axis=1,
        tiled=True,
    )
    returned = returned.reshape(slot_total, out_width)
    pair_out = returned[pair_slot].reshape(tok_count, top_count, out_width).astype(jnp.float32)
    weighted = gate_weights[:, :, None] * pair_out
    group_sum = jnp.einsum(
        "tkg,tkd->tgd", group_onehot.astype(jnp.float32), weighted, precision=lax.Precision.HIGHEST
    )
    rounded = lax.optimization_barrier(group_sum.astype(jnp.bfloat16)).astype(jnp.float32)
    routed_sum = jnp.sum(rounded, axis=1)
    mixed = shared_out + routed_sum
    return mixed.astype(jnp.bfloat16)


def column_tiles(width, tile, visit):
    whole = width // tile
    if whole == 1:
        visit(0, tile)
    elif whole > 1:

        def step(index, carry):
            visit(pl.multiple_of(index * tile, tile), tile)
            return carry

        lax.fori_loop(0, whole, step, 0)
    if width % tile:
        visit(whole * tile, width % tile)


def cube_kernel(
    sizes,
    tok_in,
    meta_in,
    wg_in,
    wu_in,
    wd_in,
    sg_in,
    su_in,
    sd_in,
    out_ref,
    tok,
    meta,
    wg,
    wu,
    wd,
    sg,
    su,
    sd,
    rows_in,
    hid_s,
    hid,
    part,
    got,
    total,
    loc_sem,
    z_send,
    z_recv,
    b_send,
    b_recv,
    m_send,
    m_recv,
    p_send,
    p_recv,
):
    ctx_count, group_count, member_count, cap = sizes
    c = lax.axis_index("ctx")
    n = lax.axis_index("node")
    l = lax.axis_index("local")
    last = ctx_count - 1
    tok_count = tok.shape[2]
    feat = tok.shape[3]
    width = wg.shape[1]
    out_width = wd.shape[1]
    slots = range(1, tok.shape[0])

    def peer(slot):
        node = n
        if slot & 1:
            node = node + 1 - 2 * lax.rem(node, 2)
        if slot & 4:
            node = lax.rem(node + group_count // 2, group_count)
        member = lax.rem(l + 1, member_count) if slot & 2 else l
        return {"node": node, "local": member}

    first = pltpu.make_async_copy(tok_in, tok.at[0, c], loc_sem.at[0])
    first.start()
    first_meta = pltpu.make_async_copy(meta_in, meta.at[0], loc_sem.at[1])
    first_meta.start()

    barrier = pltpu.get_barrier_semaphore()
    for slot in slots:
        pl.semaphore_signal(barrier, inc=1, device_id=peer(slot), device_id_type=MESH)

    @pl.when(c > 0)
    def _():
        pl.semaphore_signal(barrier, inc=1, device_id={"ctx": c - 1}, device_id_type=MESH)

    @pl.when(c < last)
    def _():
        pl.semaphore_signal(barrier, inc=1, device_id={"ctx": c + 1}, device_id_type=MESH)

    loads = []
    for index, (src, dst) in enumerate(
        ((sg_in, sg), (su_in, su), (wg_in, wg), (wu_in, wu), (sd_in, sd), (wd_in, wd))
    ):
        loads.append(pltpu.make_async_copy(src, dst, loc_sem.at[2 + index]))

    inner = (c > 0) & (c < last)

    @pl.when(inner)
    def _():
        pl.semaphore_wait(barrier, len(slots) + 2)

    @pl.when(jnp.logical_not(inner))
    def _():
        pl.semaphore_wait(barrier, len(slots) + 1)

    first.wait()
    first_meta.wait()

    def piece(chunk, shard):
        if chunk == 0:
            return tok.at[0, shard]
        if chunk == 1:
            return hid_s.at[shard]
        return hid.at[chunk - 2, shard]

    def line(chunk, depth, way, shard, target):
        return pltpu.make_async_remote_copy(
            src_ref=piece(chunk, shard),
            dst_ref=piece(chunk, shard),
            send_sem=z_send.at[way, depth, chunk],
            recv_sem=z_recv.at[way, depth, chunk],
            device_id={"ctx": target},
            device_id_type=MESH,
        )

    def line_send(chunk, depth, finish=False):
        for way in (0, 1):
            shard, target = (c - depth, c + 1) if way == 0 else (c + depth, c - 1)
            ready = (c >= depth) & (c < last) if way == 0 else (c + depth <= last) & (c > 0)

            @pl.when(ready)
            def _():
                copy = line(chunk, depth, way, shard, target)
                if finish:
                    copy.wait_send()
                else:
                    copy.start()

    def line_take(chunk, depth, then=None):
        for way in (0, 1):
            shard = c - 1 - depth if way == 0 else c + 1 + depth
            ready = shard >= 0 if way == 0 else shard <= last

            @pl.when(ready)
            def _():
                source = c - 1 if way == 0 else c + 1
                line(chunk, depth, way, shard, source).wait_recv()
                target = c + 1 if way == 0 else c - 1
                if depth < last - 1:

                    @pl.when(target < ctx_count if way == 0 else target >= 0)
                    def _():
                        line(chunk, depth + 1, way, shard, target).start()

                if then is not None:
                    then(shard)

    def hand(src_slot, dst_slot, shard, over):
        return pltpu.make_async_remote_copy(
            src_ref=tok.at[src_slot, shard],
            dst_ref=tok.at[dst_slot, shard],
            send_sem=b_send.at[dst_slot, shard],
            recv_sem=b_recv.at[dst_slot, shard],
            device_id=peer(over),
            device_id_type=MESH,
        )

    def spread(shard):
        hand(0, 2, shard, 2).start()
        hand(0, 4, shard, 4).start()
        hand(0, 1, shard, 1).start()

    line_send(0, 0)
    spread(c)
    greet = []
    for slot in slots:
        greet.append(
            pltpu.make_async_remote_copy(
                src_ref=meta.at[0],
                dst_ref=meta.at[slot],
                send_sem=m_send.at[slot],
                recv_sem=m_recv.at[slot],
                device_id=peer(slot),
                device_id_type=MESH,
            )
        )
        greet[-1].start()
    for load in loads:
        load.start()
    for depth in range(last):
        line_take(0, depth, spread)

    rank_of = lambda slot: meta[slot, pl.ds(n, 1), :]
    weight_of = lambda slot: meta[slot, pl.ds(group_count + n * member_count + l, 1), :]

    def pick(row, slot):
        spots = lax.broadcasted_iota(jnp.int32, (cap, tok_count), 0).astype(jnp.float32)
        mask = jnp.where(spots == rank_of(slot), 1.0, 0.0).astype(jnp.bfloat16)

        def step(shard, carry):
            chosen = matmul(mask, tok[slot, shard]).astype(jnp.bfloat16)
            rows_in[row : row + cap, pl.ds(pl.multiple_of(shard * feat, 128), feat)] = chosen
            return carry

        lax.fori_loop(0, ctx_count, step, 0)

    def hidden(count, gate, up, target):
        def visit(start, size):
            cols = pl.ds(start, size)
            g = matmul(rows_in[0:count, :], gate[:, cols])
            u = matmul(rows_in[0:count, :], up[:, cols])
            target[:, cols] = (g / (1.0 + jnp.exp(-g)) * u).astype(jnp.bfloat16)

        column_tiles(width, 256, visit)

    pairs = ((2, 3), (4, 5), (6, 7), (0, 1))

    def compute(index):
        for place, slot in enumerate(pairs[index]):
            pick(place * cap, slot)
        hidden(2 * cap, wg, wu, hid.at[index, c])

    half = ctx_count // 2

    def take(slot, shard):
        hand(0, slot, shard, 1).wait_recv()

    for shard in range(ctx_count):
        rows_in[0:tok_count, shard * feat : (shard + 1) * feat] = tok[0, shard]
    loads[0].wait()
    loads[1].wait()
    hidden(tok_count, sg, su, hid_s.at[c])
    line_send(1, 0)

    for shard in range(ctx_count):
        take(2, shard)
        hand(2, 3, shard, 1).start()
        if shard < half:
            hand(2, 6, shard, 4).start()
        take(4, shard)
        hand(4, 5, shard, 1).start()
        if shard >= half:
            hand(4, 6, shard, 2).start()
    for copy in greet:
        copy.wait_recv()
    loads[2].wait()
    loads[3].wait()
    for shard in range(ctx_count):
        take(1, shard)
    compute(3)
    for shard in range(ctx_count):
        take(3, shard)
    compute(0)
    line_send(2, 0)
    line_take(1, 0)
    for shard in range(ctx_count):
        take(5, shard)
    compute(1)
    line_send(3, 0)
    line_take(2, 0)
    line_take(1, 1)
    for shard in range(ctx_count):
        take(6, shard)
        hand(6, 7, shard, 1).start()
    for shard in range(ctx_count):
        take(7, shard)
    compute(2)
    line_send(4, 0)
    line_send(5, 0)
    line_take(3, 0)
    line_take(2, 1)
    line_take(1, 2)

    loads[4].wait()
    loads[5].wait()

    def product(chunk, down, cols):
        value = matmul(piece(chunk, 0)[...], down[0:width, cols])
        for shard in range(1, ctx_count):
            value = value + matmul(
                piece(chunk, shard)[...], down[shard * width : (shard + 1) * width, cols]
            )
        return value

    def shared_down(start, size):
        cols = pl.ds(start, size)
        total[:, cols] = product(1, sd, cols)

    column_tiles(out_width, 256, shared_down)

    sends = []

    def finish(index):
        weights = []
        for slot in pairs[index]:
            spots = lax.broadcasted_iota(jnp.int32, (tok_count, tok_count), 0).astype(jnp.float32)
            mask = jnp.where(spots == rank_of(slot), weight_of(slot), 0.0)
            weights.append(jnp.transpose(mask)[:, 0:cap].astype(jnp.bfloat16))

        def visit(start, size):
            cols = pl.ds(start, size)
            rows = product(index + 2, wd, cols).astype(jnp.bfloat16)
            for place, slot in enumerate(pairs[index]):
                value = matmul(weights[place], rows[place * cap : (place + 1) * cap])
                if slot == 0:
                    total[:, cols] += value
                else:
                    part[slot - 1, :, cols] = value.astype(jnp.bfloat16)

        column_tiles(out_width, 256, visit)
        for slot in pairs[index]:
            if slot:
                sends.append(
                    pltpu.make_async_remote_copy(
                        src_ref=part.at[slot - 1],
                        dst_ref=got.at[slot - 1],
                        send_sem=p_send.at[slot],
                        recv_sem=p_recv.at[slot],
                        device_id=peer(slot),
                        device_id_type=MESH,
                    )
                )
                sends[-1].start()

    line_take(4, 0)
    line_take(5, 0)
    line_take(3, 1)
    line_take(2, 2)
    finish(0)
    line_take(4, 1)
    line_take(5, 1)
    line_take(3, 2)
    finish(1)
    line_take(4, 2)
    finish(2)
    for copy in sends[:4]:
        copy.wait_recv()

    def gather_some(start, size):
        cols = pl.ds(start, size)
        value = total[:, cols]
        for slot in (2, 3, 4, 5):
            value = value + got[slot - 1, :, cols].astype(jnp.float32)
        total[:, cols] = value

    column_tiles(out_width, 256, gather_some)
    line_take(5, 2)
    finish(3)
    for copy in sends[4:]:
        copy.wait_recv()

    def gather_rest(start, size):
        cols = pl.ds(start, size)
        value = total[:, cols]
        for slot in (6, 7, 1):
            value = value + got[slot - 1, :, cols].astype(jnp.float32)
        out_ref[:, cols] = value.astype(jnp.bfloat16)

    column_tiles(out_width, 256, gather_rest)

    for copy in sends + greet:
        copy.wait_send()
    for chunk in range(6):
        for depth in range(last):
            line_send(chunk, depth, finish=True)
    for shard in range(ctx_count):
        for slot in (1, 2, 3, 4, 5, 6, 7):
            hand(0, slot, shard, 1).wait_send()


def cube(
    tokens, expert_ids, route_scores, w_gate, w_up, w_down, shared_gate, shared_up, shared_down
):
    ctx_count = lax.axis_size("ctx")
    group_count = lax.axis_size("node")
    member_count = lax.axis_size("local")
    expert_count = group_count * member_count
    tok_count, feat = tokens.shape
    cap = (10 * tok_count + 4 * group_count - 1) // (4 * group_count)
    hidden_units, out_width = w_down.shape[1:]
    width = w_gate.shape[2]
    scaled = route_scale * route_scores / jnp.sum(route_scores, axis=1, keepdims=True)
    gate_weights = lax.optimization_barrier(scaled.astype(jnp.bfloat16)).astype(jnp.float32)
    ids = expert_ids.T
    gates = gate_weights.T
    experts = jnp.arange(expert_count, dtype=jnp.int32)
    weights = jnp.sum(
        jnp.where(ids[:, None, :] == experts[None, :, None], gates[:, None, :], 0.0), axis=0
    )
    groups = jnp.arange(group_count, dtype=jnp.int32)
    member = jnp.any((ids // member_count)[:, None, :] == groups[None, :, None], axis=0)
    span = jnp.arange(tok_count, dtype=jnp.int32)
    earlier = (span[:, None] < span[None, :]).astype(jnp.bfloat16)
    rank = jnp.where(member, matmul(member.astype(jnp.bfloat16), earlier), -1.0)
    meta_rows = group_count + expert_count
    pad = -meta_rows % 8
    meta = jnp.concatenate([rank, weights, jnp.zeros((pad, tok_count), jnp.float32)], axis=0)
    slots = 2 * group_count
    bf16 = jnp.bfloat16
    rows = max(2 * cap, tok_count)
    anywhere = pl.BlockSpec(memory_space=pl.ANY)
    dma = pltpu.SemaphoreType.DMA
    kernel = lambda *refs: cube_kernel((ctx_count, group_count, member_count, cap), *refs)
    return pl.pallas_call(
        kernel,
        out_shape=jax.ShapeDtypeStruct((tok_count, out_width), bf16),
        in_specs=[anywhere] * 8,
        out_specs=pl.BlockSpec(memory_space=pltpu.VMEM),
        scratch_shapes=[
            pltpu.VMEM((slots, ctx_count, tok_count, feat), bf16),
            pltpu.VMEM((slots,) + meta.shape, jnp.float32),
            pltpu.VMEM(w_gate.shape[1:], bf16),
            pltpu.VMEM(w_up.shape[1:], bf16),
            pltpu.VMEM(w_down.shape[1:], bf16),
            pltpu.VMEM(shared_gate.shape, bf16),
            pltpu.VMEM(shared_up.shape, bf16),
            pltpu.VMEM(shared_down.shape, bf16),
            pltpu.VMEM((rows, ctx_count * feat), bf16),
            pltpu.VMEM((ctx_count, tok_count, width), bf16),
            pltpu.VMEM((4, ctx_count, 2 * cap, width), bf16),
            pltpu.VMEM((slots - 1, tok_count, out_width), bf16),
            pltpu.VMEM((slots - 1, tok_count, out_width), bf16),
            pltpu.VMEM((tok_count, out_width), jnp.float32),
            dma((8,)),
            dma((2, ctx_count - 1, 6)),
            dma((2, ctx_count - 1, 6)),
            dma((slots, ctx_count)),
            dma((slots, ctx_count)),
            dma((slots,)),
            dma((slots,)),
            dma((slots,)),
            dma((slots,)),
        ],
        compiler_params=pltpu.CompilerParams(
            collective_id=0, has_side_effects=True, vmem_limit_bytes=VMEM_BYTES
        ),
    )(
        tokens,
        meta,
        w_gate[0],
        w_up[0],
        w_down[0],
        shared_gate,
        shared_up,
        shared_down,
    )


def local(tokens, expert_ids, *rest):
    whole_groups = expert_ids.shape[1] == 2 * lax.axis_size("local")
    if whole_groups and lax.axis_size("local") == 2 and lax.axis_size("node") == 4:
        return cube(tokens, expert_ids, *rest)
    return exchange(tokens, expert_ids, *rest)


def solution(mesh):
    return jax.shard_map(
        local,
        mesh=mesh,
        in_specs=(
            P(("node", "local"), "ctx"),
            P(("node", "local"), None),
            P(("node", "local"), None),
            P(("node", "local"), None, "ctx"),
            P(("node", "local"), None, "ctx"),
            P(("node", "local"), None, "ctx"),
            P(None, "ctx"),
            P(None, "ctx"),
            P(None, "ctx"),
        ),
        out_specs=P(("node", "local"), "ctx"),
        check_vma=False,
    )
```

```python
import jax
import jax.numpy as jnp
from jax import lax
from jax.experimental import pallas as pl
from jax.experimental.pallas import tpu as pltpu
from jax.sharding import PartitionSpec as P

route_scale = 2.5
MESH = pl.DeviceIdType.MESH
VMEM_BYTES = 64000 * 1024


def matmul(left_side, right_side):
    return jnp.dot(left_side, right_side, preferred_element_type=jnp.float32)


def exchange(
    tokens, expert_ids, route_scores, w_gate, w_up, w_down, shared_gate, shared_up, shared_down
):
    tok_count = tokens.shape[0]
    feat_local = tokens.shape[1]
    top_count = expert_ids.shape[1]
    group_count = lax.axis_size("node")
    member_count = lax.axis_size("local")
    expert_count = group_count * member_count
    group_cap = (10 * tok_count + 4 * group_count - 1) // (4 * group_count)
    capacity = (2 * group_cap + member_count - 1) // member_count
    slot_total = expert_count * capacity
    gate_local = w_gate[0]
    up_local = w_up[0]
    down_local = w_down[0]
    out_width = down_local.shape[1]
    scaled = route_scale * route_scores / jnp.sum(route_scores, axis=1, keepdims=True)
    gate_weights = lax.optimization_barrier(scaled.astype(jnp.bfloat16)).astype(jnp.float32)
    group_range = jnp.arange(group_count, dtype=jnp.int32)
    group_onehot = (expert_ids // member_count)[:, :, None] == group_range[None, None, :]
    flat_ids = expert_ids.reshape(-1)
    pair_count = flat_ids.shape[0]
    onehot = (flat_ids[:, None] == jnp.arange(expert_count, dtype=jnp.int32)[None, :]).astype(
        jnp.int32
    )
    earlier = jnp.cumsum(onehot, axis=0) - onehot
    ranking = jnp.sum(earlier * onehot, axis=1)
    pair_slot = flat_ids * capacity + ranking
    pair_token = jnp.arange(pair_count, dtype=jnp.int32) // top_count
    matches = pair_slot[None, :] == jnp.arange(slot_total, dtype=jnp.int32)[:, None]
    slot_token = jnp.where(
        jnp.any(matches, axis=1),
        jnp.sum(jnp.where(matches, pair_token[None, :], 0), axis=1),
        tok_count,
    )
    padded_tokens = jnp.concatenate([tokens, jnp.zeros((1, feat_local), tokens.dtype)], axis=0)
    send_rows = padded_tokens[slot_token].reshape(group_count, member_count, capacity * feat_local)
    arrived = lax.all_to_all(
        lax.all_to_all(send_rows, "node", split_axis=0, concat_axis=0, tiled=True),
        "local",
        split_axis=1,
        concat_axis=1,
        tiled=True,
    )
    routed_rows = arrived.reshape(slot_total, feat_local)
    stacked = jnp.concatenate([routed_rows, tokens], axis=0)
    segment = lax.all_gather(stacked, "ctx", axis=1, tiled=True)
    routed_part = segment[:slot_total]
    shared_part = segment[slot_total:]
    gate_routed = matmul(routed_part, gate_local)
    up_routed = matmul(routed_part, up_local)
    gate_shared = matmul(shared_part, shared_gate)
    up_shared = matmul(shared_part, shared_up)
    routed_hidden = (jax.nn.silu(gate_routed) * up_routed).astype(jnp.bfloat16)
    shared_hidden = (jax.nn.silu(gate_shared) * up_shared).astype(jnp.bfloat16)
    hidden_stack = jnp.concatenate([routed_hidden, shared_hidden], axis=0)
    segment = lax.all_gather(hidden_stack, "ctx", axis=1, tiled=True)
    routed_out = matmul(segment[:slot_total], down_local)
    shared_out = matmul(segment[slot_total:], shared_down)
    routed_bf = routed_out.astype(jnp.bfloat16)
    sendback = routed_bf.reshape(group_count, member_count, capacity * out_width)
    returned = lax.all_to_all(
        lax.all_to_all(sendback, "node", split_axis=0, concat_axis=0, tiled=True),
        "local",
        split_axis=1,
        concat_axis=1,
        tiled=True,
    )
    returned = returned.reshape(slot_total, out_width)
    pair_out = returned[pair_slot].reshape(tok_count, top_count, out_width).astype(jnp.float32)
    weighted = gate_weights[:, :, None] * pair_out
    group_sum = jnp.einsum(
        "tkg,tkd->tgd", group_onehot.astype(jnp.float32), weighted, precision=lax.Precision.HIGHEST
    )
    rounded = lax.optimization_barrier(group_sum.astype(jnp.bfloat16)).astype(jnp.float32)
    routed_sum = jnp.sum(rounded, axis=1)
    mixed = shared_out + routed_sum
    return mixed.astype(jnp.bfloat16)


def column_tiles(width, tile, visit):
    whole = width // tile
    if whole == 1:
        visit(0, tile)
    elif whole > 1:

        def step(index, carry):
            visit(pl.multiple_of(index * tile, tile), tile)
            return carry

        lax.fori_loop(0, whole, step, 0)
    if width % tile:
        visit(whole * tile, width % tile)


def cube_kernel(
    sizes,
    tok_in,
    ids_in,
    scores_in,
    wg_in,
    wu_in,
    wd_in,
    sg_in,
    su_in,
    sd_in,
    out_ref,
    tok,
    meta,
    wg,
    wu,
    wd,
    sg,
    su,
    sd,
    rows_in,
    hid_s,
    hid,
    part,
    got,
    total,
    sum_g,
    sum_u,
    loc_sem,
    z_send,
    z_recv,
    b_send,
    b_recv,
    m_send,
    m_recv,
    p_send,
    p_recv,
):
    ctx_count, group_count, member_count, cap = sizes
    c = lax.axis_index("ctx")
    n = lax.axis_index("node")
    l = lax.axis_index("local")
    last = ctx_count - 1
    tok_count = tok.shape[2]
    feat = tok.shape[3]
    width = wg.shape[1]
    out_width = wd.shape[1]
    slots = range(1, tok.shape[0])

    def peer(slot):
        node = n
        if slot & 1:
            node = node + 1 - 2 * lax.rem(node, 2)
        if slot & 4:
            node = lax.rem(node + group_count // 2, group_count)
        member = lax.rem(l + 1, member_count) if slot & 2 else l
        return {"node": node, "local": member}

    first = pltpu.make_async_copy(tok_in, tok.at[0, c], loc_sem.at[0])
    first.start()

    barrier = pltpu.get_barrier_semaphore()
    for slot in slots:
        pl.semaphore_signal(barrier, inc=1, device_id=peer(slot), device_id_type=MESH)

    @pl.when(c > 0)
    def _():
        pl.semaphore_signal(barrier, inc=1, device_id={"ctx": c - 1}, device_id_type=MESH)

    @pl.when(c < last)
    def _():
        pl.semaphore_signal(barrier, inc=1, device_id={"ctx": c + 1}, device_id_type=MESH)

    loads = []
    for index, (src, dst) in enumerate(
        ((sg_in, sg), (su_in, su), (wg_in, wg), (wu_in, wu), (sd_in, sd), (wd_in, wd))
    ):
        loads.append(pltpu.make_async_copy(src, dst, loc_sem.at[2 + index]))

    inner = (c > 0) & (c < last)

    @pl.when(inner)
    def _():
        pl.semaphore_wait(barrier, len(slots) + 2)

    @pl.when(jnp.logical_not(inner))
    def _():
        pl.semaphore_wait(barrier, len(slots) + 1)

    first.wait()

    def piece(chunk, shard):
        if chunk == 0:
            return tok.at[0, shard]
        if chunk == 1:
            return hid_s.at[shard]
        return hid.at[chunk - 2, shard]

    def line(chunk, depth, way, shard, target):
        return pltpu.make_async_remote_copy(
            src_ref=piece(chunk, shard),
            dst_ref=piece(chunk, shard),
            send_sem=z_send.at[way, depth, chunk],
            recv_sem=z_recv.at[way, depth, chunk],
            device_id={"ctx": target},
            device_id_type=MESH,
        )

    def line_send(chunk, depth, finish=False):
        for way in (0, 1):
            shard, target = (c - depth, c + 1) if way == 0 else (c + depth, c - 1)
            ready = (c >= depth) & (c < last) if way == 0 else (c + depth <= last) & (c > 0)

            @pl.when(ready)
            def _():
                copy = line(chunk, depth, way, shard, target)
                if finish:
                    copy.wait_send()
                else:
                    copy.start()

    def line_take(chunk, depth, then=None):
        for way in (0, 1):
            shard = c - 1 - depth if way == 0 else c + 1 + depth
            ready = shard >= 0 if way == 0 else shard <= last

            @pl.when(ready)
            def _():
                source = c - 1 if way == 0 else c + 1
                line(chunk, depth, way, shard, source).wait_recv()
                target = c + 1 if way == 0 else c - 1
                if depth < last - 1:

                    @pl.when(target < ctx_count if way == 0 else target >= 0)
                    def _():
                        line(chunk, depth + 1, way, shard, target).start()

                if then is not None:
                    then(shard)

    def hand(src_slot, dst_slot, shard, over):
        return pltpu.make_async_remote_copy(
            src_ref=tok.at[src_slot, shard],
            dst_ref=tok.at[dst_slot, shard],
            send_sem=b_send.at[dst_slot, shard],
            recv_sem=b_recv.at[dst_slot, shard],
            device_id=peer(over),
            device_id_type=MESH,
        )

    def spread(shard):
        hand(0, 2, shard, 2).start()
        hand(0, 4, shard, 4).start()
        hand(0, 1, shard, 1).start()

    line_send(0, 0)
    spread(c)
    for load in loads:
        load.start()

    scores = scores_in[...]
    scaled = route_scale * scores / jnp.sum(scores, axis=1, keepdims=True)
    gates = scaled.astype(jnp.bfloat16).astype(jnp.float32)
    lane = lax.broadcasted_iota(jnp.int32, (tok_count, tok_count), 1)
    named = jnp.zeros((tok_count, tok_count), jnp.float32)
    for k in range(ids_in.shape[1]):
        expert = ids_in[:, k : k + 1]
        named = jnp.maximum(named, jnp.where(lane == expert // member_count, 1.0, 0.0))
    table = jnp.where(lane < group_count, named, 0.0)
    for k in range(ids_in.shape[1]):
        expert = ids_in[:, k : k + 1]
        table = table + jnp.where(lane == expert + group_count, gates[:, k : k + 1], 0.0)
    table = jnp.transpose(table)[0 : meta.shape[1]]
    before = lax.broadcasted_iota(jnp.int32, (tok_count, tok_count), 0) < lane
    counts = matmul(table.astype(jnp.bfloat16), jnp.where(before, 1.0, 0.0).astype(jnp.bfloat16))
    row = lax.broadcasted_iota(jnp.int32, table.shape, 0)
    meta[0] = jnp.where(row < group_count, jnp.where(table > 0.5, counts, -1.0), table)

    greet = []
    for slot in slots:
        greet.append(
            pltpu.make_async_remote_copy(
                src_ref=meta.at[0],
                dst_ref=meta.at[slot],
                send_sem=m_send.at[slot],
                recv_sem=m_recv.at[slot],
                device_id=peer(slot),
                device_id_type=MESH,
            )
        )
        greet[-1].start()

    def shared_add(shard, fresh=False):
        ins = pl.ds(pl.multiple_of(shard * feat, 128), feat)

        def visit(start, size):
            cols = pl.ds(start, size)
            g = matmul(tok[0, shard], sg[ins, cols])
            u = matmul(tok[0, shard], su[ins, cols])
            sum_g[:, cols] = g if fresh else sum_g[:, cols] + g
            sum_u[:, cols] = u if fresh else sum_u[:, cols] + u

        column_tiles(width, 256, visit)

    loads[0].wait()
    loads[1].wait()
    shared_add(c, True)
    for depth in range(last):
        line_take(0, depth, spread)
        for shard in (c - 1 - depth, c + 1 + depth):

            @pl.when((shard >= 0) & (shard <= last))
            def _():
                shared_add(shard)


    rank_of = lambda slot: meta[slot, pl.ds(n, 1), :]
    weight_of = lambda slot: meta[slot, pl.ds(group_count + n * member_count + l, 1), :]

    def pick(row, slot):
        spots = lax.broadcasted_iota(jnp.int32, (cap, tok_count), 0).astype(jnp.float32)
        mask = jnp.where(spots == rank_of(slot), 1.0, 0.0).astype(jnp.bfloat16)

        def step(shard, carry):
            chosen = matmul(mask, tok[slot, shard]).astype(jnp.bfloat16)
            rows_in[row : row + cap, pl.ds(pl.multiple_of(shard * feat, 128), feat)] = chosen
            return carry

        lax.fori_loop(0, ctx_count, step, 0)

    def hidden(count, gate, up, target):
        def visit(start, size):
            cols = pl.ds(start, size)
            g = matmul(rows_in[0:count, :], gate[:, cols])
            u = matmul(rows_in[0:count, :], up[:, cols])
            target[:, cols] = (g / (1.0 + jnp.exp(-g)) * u).astype(jnp.bfloat16)

        column_tiles(width, 256, visit)

    pairs = ((2, 3), (4, 5), (6, 7), (0, 1))

    def compute(index):
        for place, slot in enumerate(pairs[index]):
            pick(place * cap, slot)
        hidden(2 * cap, wg, wu, hid.at[index, c])

    half = ctx_count // 2

    def take(slot, shard):
        hand(0, slot, shard, 1).wait_recv()

    g = sum_g[...]
    hid_s[c] = (g / (1.0 + jnp.exp(-g)) * sum_u[...]).astype(jnp.bfloat16)
    line_send(1, 0)

    for copy in greet:
        copy.wait_recv()
    loads[2].wait()
    loads[3].wait()
    for shard in range(ctx_count):
        take(1, shard)
    compute(3)
    line_take(1, 0)
    for shard in range(ctx_count):
        take(2, shard)
        hand(2, 3, shard, 1).start()
        if shard < half:
            hand(2, 6, shard, 4).start()
        take(4, shard)
        hand(4, 5, shard, 1).start()
        if shard >= half:
            hand(4, 6, shard, 2).start()
    for shard in range(ctx_count):
        take(3, shard)
    compute(0)
    line_send(2, 0)
    line_take(1, 1)
    for shard in range(ctx_count):
        take(5, shard)
    compute(1)
    line_send(3, 0)
    line_take(2, 0)
    line_take(1, 2)

    loads[4].wait()
    loads[5].wait()

    def product(chunk, down, cols):
        value = matmul(piece(chunk, 0)[...], down[0:width, cols])
        for shard in range(1, ctx_count):
            value = value + matmul(
                piece(chunk, shard)[...], down[shard * width : (shard + 1) * width, cols]
            )
        return value

    def shared_down(start, size):
        cols = pl.ds(start, size)
        total[:, cols] = product(1, sd, cols)

    column_tiles(out_width, 256, shared_down)

    sends = []

    def finish(index):
        weights = []
        for slot in pairs[index]:
            spots = lax.broadcasted_iota(jnp.int32, (tok_count, tok_count), 0).astype(jnp.float32)
            mask = jnp.where(spots == rank_of(slot), weight_of(slot), 0.0)
            weights.append(jnp.transpose(mask)[:, 0:cap].astype(jnp.bfloat16))

        def visit(start, size):
            cols = pl.ds(start, size)
            rows = product(index + 2, wd, cols).astype(jnp.bfloat16)
            for place, slot in enumerate(pairs[index]):
                value = matmul(weights[place], rows[place * cap : (place + 1) * cap])
                if slot == 0:
                    total[:, cols] += value
                else:
                    part[slot - 1, :, cols] = value.astype(jnp.bfloat16)

        column_tiles(out_width, 256, visit)
        for slot in pairs[index]:
            if slot:
                sends.append(
                    pltpu.make_async_remote_copy(
                        src_ref=part.at[slot - 1],
                        dst_ref=got.at[slot - 1],
                        send_sem=p_send.at[slot],
                        recv_sem=p_recv.at[slot],
                        device_id=peer(slot),
                        device_id_type=MESH,
                    )
                )
                sends[-1].start()

    for shard in range(ctx_count):
        take(6, shard)
        hand(6, 7, shard, 1).start()
    line_take(2, 1)
    for shard in range(ctx_count):
        take(7, shard)
    compute(2)
    line_send(4, 0)
    line_take(3, 0)
    line_take(3, 1)
    line_take(2, 2)
    finish(0)
    line_send(5, 0)
    line_take(4, 0)
    line_take(4, 1)
    line_take(3, 2)
    finish(1)
    line_take(5, 0)
    line_take(5, 1)
    line_take(4, 2)
    finish(2)
    for copy in sends[:4]:
        copy.wait_recv()

    def gather_some(start, size):
        cols = pl.ds(start, size)
        value = total[:, cols]
        for slot in (2, 3, 4, 5):
            value = value + got[slot - 1, :, cols].astype(jnp.float32)
        total[:, cols] = value

    column_tiles(out_width, 256, gather_some)
    line_take(5, 2)
    finish(3)
    for copy in sends[4:]:
        copy.wait_recv()

    def gather_rest(start, size):
        cols = pl.ds(start, size)
        value = total[:, cols]
        for slot in (6, 7, 1):
            value = value + got[slot - 1, :, cols].astype(jnp.float32)
        out_ref[:, cols] = value.astype(jnp.bfloat16)

    column_tiles(out_width, 256, gather_rest)

    for copy in sends + greet:
        copy.wait_send()
    for chunk in range(6):
        for depth in range(last):
            line_send(chunk, depth, finish=True)
    for shard in range(ctx_count):
        for slot in (1, 2, 3, 4, 5, 6, 7):
            hand(0, slot, shard, 1).wait_send()


def cube(
    tokens, expert_ids, route_scores, w_gate, w_up, w_down, shared_gate, shared_up, shared_down
):
    ctx_count = lax.axis_size("ctx")
    group_count = lax.axis_size("node")
    member_count = lax.axis_size("local")
    expert_count = group_count * member_count
    tok_count, feat = tokens.shape
    cap = (10 * tok_count + 4 * group_count - 1) // (4 * group_count)
    hidden_units, out_width = w_down.shape[1:]
    width = w_gate.shape[2]
    meta_rows = -(-(group_count + expert_count) // 16) * 16
    slots = 2 * group_count
    bf16 = jnp.bfloat16
    rows = max(2 * cap, tok_count)
    anywhere = pl.BlockSpec(memory_space=pl.ANY)
    inside = pl.BlockSpec(memory_space=pltpu.VMEM)
    dma = pltpu.SemaphoreType.DMA
    kernel = lambda *refs: cube_kernel((ctx_count, group_count, member_count, cap), *refs)
    return pl.pallas_call(
        kernel,
        out_shape=jax.ShapeDtypeStruct((tok_count, out_width), bf16),
        in_specs=[anywhere, inside, inside] + [anywhere] * 6,
        out_specs=inside,
        scratch_shapes=[
            pltpu.VMEM((slots, ctx_count, tok_count, feat), bf16),
            pltpu.VMEM((slots, meta_rows, tok_count), jnp.float32),
            pltpu.VMEM(w_gate.shape[1:], bf16),
            pltpu.VMEM(w_up.shape[1:], bf16),
            pltpu.VMEM(w_down.shape[1:], bf16),
            pltpu.VMEM(shared_gate.shape, bf16),
            pltpu.VMEM(shared_up.shape, bf16),
            pltpu.VMEM(shared_down.shape, bf16),
            pltpu.VMEM((rows, ctx_count * feat), bf16),
            pltpu.VMEM((ctx_count, tok_count, width), bf16),
            pltpu.VMEM((4, ctx_count, 2 * cap, width), bf16),
            pltpu.VMEM((slots - 1, tok_count, out_width), bf16),
            pltpu.VMEM((slots - 1, tok_count, out_width), bf16),
            pltpu.VMEM((tok_count, out_width), jnp.float32),
            pltpu.VMEM((tok_count, width), jnp.float32),
            pltpu.VMEM((tok_count, width), jnp.float32),
            dma((8,)),
            dma((2, ctx_count - 1, 6)),
            dma((2, ctx_count - 1, 6)),
            dma((slots, ctx_count)),
            dma((slots, ctx_count)),
            dma((slots,)),
            dma((slots,)),
            dma((slots,)),
            dma((slots,)),
        ],
        compiler_params=pltpu.CompilerParams(
            collective_id=0, has_side_effects=True, vmem_limit_bytes=VMEM_BYTES
        ),
    )(
        tokens,
        expert_ids,
        route_scores,
        w_gate[0],
        w_up[0],
        w_down[0],
        shared_gate,
        shared_up,
        shared_down,
    )


def local(tokens, expert_ids, *rest):
    whole_groups = expert_ids.shape[1] == 2 * lax.axis_size("local")
    if whole_groups and lax.axis_size("local") == 2 and lax.axis_size("node") == 4:
        return cube(tokens, expert_ids, *rest)
    return exchange(tokens, expert_ids, *rest)


def solution(mesh):
    return jax.shard_map(
        local,
        mesh=mesh,
        in_specs=(
            P(("node", "local"), "ctx"),
            P(("node", "local"), None),
            P(("node", "local"), None),
            P(("node", "local"), None, "ctx"),
            P(("node", "local"), None, "ctx"),
            P(("node", "local"), None, "ctx"),
            P(None, "ctx"),
            P(None, "ctx"),
            P(None, "ctx"),
        ),
        out_specs=P(("node", "local"), "ctx"),
        check_vma=False,
    )
```

```python
import jax
import jax.numpy as jnp
from jax import lax
from jax.experimental import pallas as pl
from jax.experimental.pallas import tpu as pltpu
from jax.sharding import PartitionSpec as P

route_scale = 2.5
MESH = pl.DeviceIdType.MESH
VMEM_BYTES = 64000 * 1024


def matmul(left_side, right_side):
    return jnp.dot(left_side, right_side, preferred_element_type=jnp.float32)


def exchange(
    tokens, expert_ids, route_scores, w_gate, w_up, w_down, shared_gate, shared_up, shared_down
):
    tok_count = tokens.shape[0]
    feat_local = tokens.shape[1]
    top_count = expert_ids.shape[1]
    group_count = lax.axis_size("node")
    member_count = lax.axis_size("local")
    expert_count = group_count * member_count
    group_cap = (10 * tok_count + 4 * group_count - 1) // (4 * group_count)
    capacity = (2 * group_cap + member_count - 1) // member_count
    slot_total = expert_count * capacity
    gate_local = w_gate[0]
    up_local = w_up[0]
    down_local = w_down[0]
    out_width = down_local.shape[1]
    scaled = route_scale * route_scores / jnp.sum(route_scores, axis=1, keepdims=True)
    gate_weights = lax.optimization_barrier(scaled.astype(jnp.bfloat16)).astype(jnp.float32)
    group_range = jnp.arange(group_count, dtype=jnp.int32)
    group_onehot = (expert_ids // member_count)[:, :, None] == group_range[None, None, :]
    flat_ids = expert_ids.reshape(-1)
    pair_count = flat_ids.shape[0]
    onehot = (flat_ids[:, None] == jnp.arange(expert_count, dtype=jnp.int32)[None, :]).astype(
        jnp.int32
    )
    earlier = jnp.cumsum(onehot, axis=0) - onehot
    ranking = jnp.sum(earlier * onehot, axis=1)
    pair_slot = flat_ids * capacity + ranking
    pair_token = jnp.arange(pair_count, dtype=jnp.int32) // top_count
    matches = pair_slot[None, :] == jnp.arange(slot_total, dtype=jnp.int32)[:, None]
    slot_token = jnp.where(
        jnp.any(matches, axis=1),
        jnp.sum(jnp.where(matches, pair_token[None, :], 0), axis=1),
        tok_count,
    )
    padded_tokens = jnp.concatenate([tokens, jnp.zeros((1, feat_local), tokens.dtype)], axis=0)
    send_rows = padded_tokens[slot_token].reshape(group_count, member_count, capacity * feat_local)
    arrived = lax.all_to_all(
        lax.all_to_all(send_rows, "node", split_axis=0, concat_axis=0, tiled=True),
        "local",
        split_axis=1,
        concat_axis=1,
        tiled=True,
    )
    routed_rows = arrived.reshape(slot_total, feat_local)
    stacked = jnp.concatenate([routed_rows, tokens], axis=0)
    segment = lax.all_gather(stacked, "ctx", axis=1, tiled=True)
    routed_part = segment[:slot_total]
    shared_part = segment[slot_total:]
    gate_routed = matmul(routed_part, gate_local)
    up_routed = matmul(routed_part, up_local)
    gate_shared = matmul(shared_part, shared_gate)
    up_shared = matmul(shared_part, shared_up)
    routed_hidden = (jax.nn.silu(gate_routed) * up_routed).astype(jnp.bfloat16)
    shared_hidden = (jax.nn.silu(gate_shared) * up_shared).astype(jnp.bfloat16)
    hidden_stack = jnp.concatenate([routed_hidden, shared_hidden], axis=0)
    segment = lax.all_gather(hidden_stack, "ctx", axis=1, tiled=True)
    routed_out = matmul(segment[:slot_total], down_local)
    shared_out = matmul(segment[slot_total:], shared_down)
    routed_bf = routed_out.astype(jnp.bfloat16)
    sendback = routed_bf.reshape(group_count, member_count, capacity * out_width)
    returned = lax.all_to_all(
        lax.all_to_all(sendback, "node", split_axis=0, concat_axis=0, tiled=True),
        "local",
        split_axis=1,
        concat_axis=1,
        tiled=True,
    )
    returned = returned.reshape(slot_total, out_width)
    pair_out = returned[pair_slot].reshape(tok_count, top_count, out_width).astype(jnp.float32)
    weighted = gate_weights[:, :, None] * pair_out
    group_sum = jnp.einsum(
        "tkg,tkd->tgd", group_onehot.astype(jnp.float32), weighted, precision=lax.Precision.HIGHEST
    )
    rounded = lax.optimization_barrier(group_sum.astype(jnp.bfloat16)).astype(jnp.float32)
    routed_sum = jnp.sum(rounded, axis=1)
    mixed = shared_out + routed_sum
    return mixed.astype(jnp.bfloat16)


def column_tiles(width, tile, visit):
    whole = width // tile
    if whole == 1:
        visit(0, tile)
    elif whole > 1:

        def step(index, carry):
            visit(pl.multiple_of(index * tile, tile), tile)
            return carry

        lax.fori_loop(0, whole, step, 0)
    if width % tile:
        visit(whole * tile, width % tile)


def cube_kernel(
    sizes,
    tok_in,
    ids_in,
    scores_in,
    wg_in,
    wu_in,
    wd_in,
    sg_in,
    su_in,
    sd_in,
    out_ref,
    tok,
    meta,
    wg,
    wu,
    wd,
    sg,
    su,
    sd,
    rows_in,
    hid_s,
    hid,
    part,
    got,
    total,
    sum_g,
    sum_u,
    hold,
    loc_sem,
    z_send,
    z_recv,
    b_send,
    b_recv,
    m_send,
    m_recv,
    p_send,
    p_recv,
):
    ctx_count, group_count, member_count, cap = sizes
    c = lax.axis_index("ctx")
    n = lax.axis_index("node")
    l = lax.axis_index("local")
    last = ctx_count - 1
    tok_count = tok.shape[2]
    feat = tok.shape[3]
    width = wg.shape[1]
    out_width = wd.shape[1]
    slots = range(1, tok.shape[0])

    def peer(slot):
        node = n
        if slot & 1:
            node = node + 1 - 2 * lax.rem(node, 2)
        if slot & 4:
            node = lax.rem(node + group_count // 2, group_count)
        member = lax.rem(l + 1, member_count) if slot & 2 else l
        return {"node": node, "local": member}

    first = pltpu.make_async_copy(tok_in, tok.at[0, c], loc_sem.at[0])
    first.start()

    barrier = pltpu.get_barrier_semaphore()
    for slot in slots:
        pl.semaphore_signal(barrier, inc=1, device_id=peer(slot), device_id_type=MESH)

    @pl.when(c > 0)
    def _():
        pl.semaphore_signal(barrier, inc=1, device_id={"ctx": c - 1}, device_id_type=MESH)

    @pl.when(c < last)
    def _():
        pl.semaphore_signal(barrier, inc=1, device_id={"ctx": c + 1}, device_id_type=MESH)

    loads = []
    for index, (src, dst) in enumerate(
        ((sg_in, sg), (su_in, su), (wg_in, wg), (wu_in, wu), (sd_in, sd), (wd_in, wd))
    ):
        loads.append(pltpu.make_async_copy(src, dst, loc_sem.at[2 + index]))

    inner = (c > 0) & (c < last)

    @pl.when(inner)
    def _():
        pl.semaphore_wait(barrier, len(slots) + 2)

    @pl.when(jnp.logical_not(inner))
    def _():
        pl.semaphore_wait(barrier, len(slots) + 1)

    first.wait()

    def piece(chunk, shard):
        if chunk == 0:
            return tok.at[0, shard]
        if chunk == 1:
            return hid_s.at[shard]
        return hid.at[chunk - 2, shard]

    def line(chunk, depth, way, shard, target):
        return pltpu.make_async_remote_copy(
            src_ref=piece(chunk, shard),
            dst_ref=piece(chunk, shard),
            send_sem=z_send.at[way, depth, chunk],
            recv_sem=z_recv.at[way, depth, chunk],
            device_id={"ctx": target},
            device_id_type=MESH,
        )

    def line_send(chunk, depth, finish=False):
        for way in (0, 1):
            shard, target = (c - depth, c + 1) if way == 0 else (c + depth, c - 1)
            ready = (c >= depth) & (c < last) if way == 0 else (c + depth <= last) & (c > 0)

            @pl.when(ready)
            def _():
                copy = line(chunk, depth, way, shard, target)
                if finish:
                    copy.wait_send()
                else:
                    copy.start()

    def line_take(chunk, depth, then=None):
        for way in (0, 1):
            shard = c - 1 - depth if way == 0 else c + 1 + depth
            ready = shard >= 0 if way == 0 else shard <= last

            @pl.when(ready)
            def _():
                source = c - 1 if way == 0 else c + 1
                line(chunk, depth, way, shard, source).wait_recv()
                target = c + 1 if way == 0 else c - 1
                if depth < last - 1:

                    @pl.when(target < ctx_count if way == 0 else target >= 0)
                    def _():
                        line(chunk, depth + 1, way, shard, target).start()

                if then is not None:
                    then(shard)

    def hand(src_slot, dst_slot, shard, over):
        return pltpu.make_async_remote_copy(
            src_ref=tok.at[src_slot, shard],
            dst_ref=tok.at[dst_slot, shard],
            send_sem=b_send.at[dst_slot, shard],
            recv_sem=b_recv.at[dst_slot, shard],
            device_id=peer(over),
            device_id_type=MESH,
        )

    def spread(shard):
        hand(0, 2, shard, 2).start()
        hand(0, 4, shard, 4).start()
        hand(0, 1, shard, 1).start()

    line_send(0, 0)
    spread(c)
    for load in loads:
        load.start()

    scores = scores_in[...]
    scaled = route_scale * scores / jnp.sum(scores, axis=0, keepdims=True)
    gates = scaled.astype(jnp.bfloat16).astype(jnp.float32)
    row = lax.broadcasted_iota(jnp.int32, meta.shape[1:], 0)
    named = jnp.zeros(row.shape, jnp.float32)
    table = jnp.zeros(row.shape, jnp.float32)
    for k in range(ids_in.shape[0]):
        expert = ids_in[k : k + 1, :]
        named = jnp.where(row == expert // member_count, 1.0, named)
        table = table + jnp.where(row == expert + group_count, gates[k : k + 1, :], 0.0)
    square = (tok_count, tok_count)
    before = lax.broadcasted_iota(jnp.int32, square, 0) < lax.broadcasted_iota(jnp.int32, square, 1)
    counts = matmul(named.astype(jnp.bfloat16), jnp.where(before, 1.0, 0.0).astype(jnp.bfloat16))
    meta[0] = jnp.where(row < group_count, jnp.where(named > 0.5, counts, -1.0), table)

    greet = []
    for slot in slots:
        greet.append(
            pltpu.make_async_remote_copy(
                src_ref=meta.at[0],
                dst_ref=meta.at[slot],
                send_sem=m_send.at[slot],
                recv_sem=m_recv.at[slot],
                device_id=peer(slot),
                device_id_type=MESH,
            )
        )
        greet[-1].start()

    def shared_add(shard, fresh=False):
        ins = pl.ds(pl.multiple_of(shard * feat, 128), feat)

        def visit(start, size):
            cols = pl.ds(start, size)
            g = matmul(tok[0, shard], sg[ins, cols])
            u = matmul(tok[0, shard], su[ins, cols])
            sum_g[:, cols] = g if fresh else sum_g[:, cols] + g
            sum_u[:, cols] = u if fresh else sum_u[:, cols] + u

        column_tiles(width, 256, visit)

    loads[0].wait()
    loads[1].wait()
    shared_add(c, True)
    for depth in range(last):
        line_take(0, depth, spread)
        for shard in (c - 1 - depth, c + 1 + depth):

            @pl.when((shard >= 0) & (shard <= last))
            def _():
                shared_add(shard)


    rank_of = lambda slot: meta[slot, pl.ds(n, 1), :]
    weight_of = lambda slot: meta[slot, pl.ds(group_count + n * member_count + l, 1), :]

    def pick(row, slot):
        spots = lax.broadcasted_iota(jnp.int32, (cap, tok_count), 0).astype(jnp.float32)
        mask = jnp.where(spots == rank_of(slot), 1.0, 0.0).astype(jnp.bfloat16)

        def step(shard, carry):
            chosen = matmul(mask, tok[slot, shard]).astype(jnp.bfloat16)
            rows_in[row : row + cap, pl.ds(pl.multiple_of(shard * feat, 128), feat)] = chosen
            return carry

        lax.fori_loop(0, ctx_count, step, 0)

    def hidden(count, gate, up, target):
        def visit(start, size):
            cols = pl.ds(start, size)
            g = matmul(rows_in[0:count, :], gate[:, cols])
            u = matmul(rows_in[0:count, :], up[:, cols])
            target[:, cols] = (g / (1.0 + jnp.exp(-g)) * u).astype(jnp.bfloat16)

        column_tiles(width, 256, visit)

    pairs = ((2, 3), (4, 5), (6, 7), (0, 1))

    def compute(index):
        for place, slot in enumerate(pairs[index]):
            pick(place * cap, slot)
        hidden(2 * cap, wg, wu, hid.at[index, c])

    half = ctx_count // 2

    def take(slot, shard):
        hand(0, slot, shard, 1).wait_recv()

    g = sum_g[...]
    hid_s[c] = (g / (1.0 + jnp.exp(-g)) * sum_u[...]).astype(jnp.bfloat16)
    line_send(1, 0)

    for copy in greet:
        copy.wait_recv()
    loads[2].wait()
    loads[3].wait()
    for shard in range(ctx_count):
        take(1, shard)
    compute(3)
    line_take(1, 0)
    for shard in range(ctx_count):
        take(2, shard)
        hand(2, 3, shard, 1).start()
        if shard < half:
            hand(2, 6, shard, 4).start()
        take(4, shard)
        hand(4, 5, shard, 1).start()
        if shard >= half:
            hand(4, 6, shard, 2).start()
    for shard in range(ctx_count):
        take(3, shard)
    compute(0)
    line_send(2, 0)
    line_take(1, 1)
    for shard in range(ctx_count):
        take(5, shard)
    compute(1)
    line_send(3, 0)
    line_take(2, 0)
    line_take(1, 2)

    loads[4].wait()
    loads[5].wait()

    def product(chunk, down, cols):
        value = matmul(piece(chunk, 0)[...], down[0:width, cols])
        for shard in range(1, ctx_count):
            value = value + matmul(
                piece(chunk, shard)[...], down[shard * width : (shard + 1) * width, cols]
            )
        return value

    def shared_down(start, size):
        cols = pl.ds(start, size)
        total[:, cols] = product(1, sd, cols)

    column_tiles(out_width, 256, shared_down)

    sends = {}

    def ship(slot, over):
        sends[slot] = pltpu.make_async_remote_copy(
            src_ref=part.at[slot - 1],
            dst_ref=got.at[slot - 1],
            send_sem=p_send.at[slot],
            recv_sem=p_recv.at[slot],
            device_id=peer(over),
            device_id_type=MESH,
        )
        sends[slot].start()

    def finish(index):
        weights = []
        for slot in pairs[index]:
            spots = lax.broadcasted_iota(jnp.int32, (tok_count, tok_count), 0).astype(jnp.float32)
            mask = jnp.where(spots == rank_of(slot), weight_of(slot), 0.0)
            weights.append(jnp.transpose(mask)[:, 0:cap].astype(jnp.bfloat16))

        def visit(start, size):
            cols = pl.ds(start, size)
            rows = product(index + 2, wd, cols).astype(jnp.bfloat16)
            for place, slot in enumerate(pairs[index]):
                value = matmul(weights[place], rows[place * cap : (place + 1) * cap])
                if slot == 0:
                    total[:, cols] += value
                elif place == 0:
                    hold[:, cols] = value
                else:
                    part[slot - 1, :, cols] = value.astype(jnp.bfloat16)

        column_tiles(out_width, 256, visit)
        ship(pairs[index][1], 1)

    def forward(index):
        slot, other = pairs[index]
        sends[other].wait_recv()

        def visit(start, size):
            cols = pl.ds(start, size)
            value = hold[:, cols] + got[other - 1, :, cols].astype(jnp.float32)
            part[slot - 1, :, cols] = value.astype(jnp.bfloat16)

        column_tiles(out_width, 256, visit)
        ship(slot, slot)

    for shard in range(ctx_count):
        take(6, shard)
        hand(6, 7, shard, 1).start()
    line_take(2, 1)
    for shard in range(ctx_count):
        take(7, shard)
    compute(2)
    line_send(4, 0)
    line_take(3, 0)
    line_take(3, 1)
    line_take(2, 2)
    finish(0)
    line_send(5, 0)
    line_take(4, 0)
    forward(0)
    line_take(4, 1)
    line_take(3, 2)
    finish(1)
    line_take(5, 0)
    forward(1)
    line_take(5, 1)
    line_take(4, 2)
    finish(2)
    forward(2)
    for slot in (2, 4):
        sends[slot].wait_recv()

    def gather_some(start, size):
        cols = pl.ds(start, size)
        value = total[:, cols]
        for slot in (2, 4):
            value = value + got[slot - 1, :, cols].astype(jnp.float32)
        total[:, cols] = value

    column_tiles(out_width, 256, gather_some)
    line_take(5, 2)
    finish(3)
    for slot in (6, 1):
        sends[slot].wait_recv()

    def gather_rest(start, size):
        cols = pl.ds(start, size)
        value = total[:, cols]
        for slot in (6, 1):
            value = value + got[slot - 1, :, cols].astype(jnp.float32)
        out_ref[:, cols] = value.astype(jnp.bfloat16)

    column_tiles(out_width, 256, gather_rest)

    for copy in list(sends.values()) + greet:
        copy.wait_send()
    for chunk in range(6):
        for depth in range(last):
            line_send(chunk, depth, finish=True)
    for shard in range(ctx_count):
        for slot in (1, 2, 3, 4, 5, 6, 7):
            hand(0, slot, shard, 1).wait_send()


def cube(
    tokens, expert_ids, route_scores, w_gate, w_up, w_down, shared_gate, shared_up, shared_down
):
    ctx_count = lax.axis_size("ctx")
    group_count = lax.axis_size("node")
    member_count = lax.axis_size("local")
    expert_count = group_count * member_count
    tok_count, feat = tokens.shape
    cap = (10 * tok_count + 4 * group_count - 1) // (4 * group_count)
    hidden_units, out_width = w_down.shape[1:]
    width = w_gate.shape[2]
    meta_rows = -(-(group_count + expert_count) // 16) * 16
    slots = 2 * group_count
    bf16 = jnp.bfloat16
    rows = max(2 * cap, tok_count)
    anywhere = pl.BlockSpec(memory_space=pl.ANY)
    inside = pl.BlockSpec(memory_space=pltpu.VMEM)
    dma = pltpu.SemaphoreType.DMA
    kernel = lambda *refs: cube_kernel((ctx_count, group_count, member_count, cap), *refs)
    return pl.pallas_call(
        kernel,
        out_shape=jax.ShapeDtypeStruct((tok_count, out_width), bf16),
        in_specs=[anywhere, inside, inside] + [anywhere] * 6,
        out_specs=inside,
        scratch_shapes=[
            pltpu.VMEM((slots, ctx_count, tok_count, feat), bf16),
            pltpu.VMEM((slots, meta_rows, tok_count), jnp.float32),
            pltpu.VMEM(w_gate.shape[1:], bf16),
            pltpu.VMEM(w_up.shape[1:], bf16),
            pltpu.VMEM(w_down.shape[1:], bf16),
            pltpu.VMEM(shared_gate.shape, bf16),
            pltpu.VMEM(shared_up.shape, bf16),
            pltpu.VMEM(shared_down.shape, bf16),
            pltpu.VMEM((rows, ctx_count * feat), bf16),
            pltpu.VMEM((ctx_count, tok_count, width), bf16),
            pltpu.VMEM((4, ctx_count, 2 * cap, width), bf16),
            pltpu.VMEM((slots - 1, tok_count, out_width), bf16),
            pltpu.VMEM((slots - 1, tok_count, out_width), bf16),
            pltpu.VMEM((tok_count, out_width), jnp.float32),
            pltpu.VMEM((tok_count, width), jnp.float32),
            pltpu.VMEM((tok_count, width), jnp.float32),
            pltpu.VMEM((tok_count, out_width), jnp.float32),
            dma((8,)),
            dma((2, ctx_count - 1, 6)),
            dma((2, ctx_count - 1, 6)),
            dma((slots, ctx_count)),
            dma((slots, ctx_count)),
            dma((slots,)),
            dma((slots,)),
            dma((slots,)),
            dma((slots,)),
        ],
        compiler_params=pltpu.CompilerParams(
            collective_id=0, has_side_effects=True, vmem_limit_bytes=VMEM_BYTES
        ),
    )(
        tokens,
        expert_ids.T,
        route_scores.T,
        w_gate[0],
        w_up[0],
        w_down[0],
        shared_gate,
        shared_up,
        shared_down,
    )


def local(tokens, expert_ids, *rest):
    whole_groups = expert_ids.shape[1] == 2 * lax.axis_size("local")
    if whole_groups and lax.axis_size("local") == 2 and lax.axis_size("node") == 4:
        return cube(tokens, expert_ids, *rest)
    return exchange(tokens, expert_ids, *rest)


def solution(mesh):
    return jax.shard_map(
        local,
        mesh=mesh,
        in_specs=(
            P(("node", "local"), "ctx"),
            P(("node", "local"), None),
            P(("node", "local"), None),
            P(("node", "local"), None, "ctx"),
            P(("node", "local"), None, "ctx"),
            P(("node", "local"), None, "ctx"),
            P(None, "ctx"),
            P(None, "ctx"),
            P(None, "ctx"),
        ),
        out_specs=P(("node", "local"), "ctx"),
        check_vma=False,
    )
```

```python
import jax
import jax.numpy as jnp
from jax import lax
from jax.experimental import pallas as pl
from jax.experimental.pallas import tpu as pltpu
from jax.sharding import PartitionSpec as P

route_scale = 2.5
MESH = pl.DeviceIdType.MESH
VMEM_BYTES = 64000 * 1024


def matmul(left_side, right_side):
    return jnp.dot(left_side, right_side, preferred_element_type=jnp.float32)


def exchange(
    tokens, expert_ids, route_scores, w_gate, w_up, w_down, shared_gate, shared_up, shared_down
):
    tok_count = tokens.shape[0]
    feat_local = tokens.shape[1]
    top_count = expert_ids.shape[1]
    group_count = lax.axis_size("node")
    member_count = lax.axis_size("local")
    expert_count = group_count * member_count
    group_cap = (10 * tok_count + 4 * group_count - 1) // (4 * group_count)
    capacity = (2 * group_cap + member_count - 1) // member_count
    slot_total = expert_count * capacity
    gate_local = w_gate[0]
    up_local = w_up[0]
    down_local = w_down[0]
    out_width = down_local.shape[1]
    scaled = route_scale * route_scores / jnp.sum(route_scores, axis=1, keepdims=True)
    gate_weights = lax.optimization_barrier(scaled.astype(jnp.bfloat16)).astype(jnp.float32)
    group_range = jnp.arange(group_count, dtype=jnp.int32)
    group_onehot = (expert_ids // member_count)[:, :, None] == group_range[None, None, :]
    flat_ids = expert_ids.reshape(-1)
    pair_count = flat_ids.shape[0]
    onehot = (flat_ids[:, None] == jnp.arange(expert_count, dtype=jnp.int32)[None, :]).astype(
        jnp.int32
    )
    earlier = jnp.cumsum(onehot, axis=0) - onehot
    ranking = jnp.sum(earlier * onehot, axis=1)
    pair_slot = flat_ids * capacity + ranking
    pair_token = jnp.arange(pair_count, dtype=jnp.int32) // top_count
    matches = pair_slot[None, :] == jnp.arange(slot_total, dtype=jnp.int32)[:, None]
    slot_token = jnp.where(
        jnp.any(matches, axis=1),
        jnp.sum(jnp.where(matches, pair_token[None, :], 0), axis=1),
        tok_count,
    )
    padded_tokens = jnp.concatenate([tokens, jnp.zeros((1, feat_local), tokens.dtype)], axis=0)
    send_rows = padded_tokens[slot_token].reshape(group_count, member_count, capacity * feat_local)
    arrived = lax.all_to_all(
        lax.all_to_all(send_rows, "node", split_axis=0, concat_axis=0, tiled=True),
        "local",
        split_axis=1,
        concat_axis=1,
        tiled=True,
    )
    routed_rows = arrived.reshape(slot_total, feat_local)
    stacked = jnp.concatenate([routed_rows, tokens], axis=0)
    segment = lax.all_gather(stacked, "ctx", axis=1, tiled=True)
    routed_part = segment[:slot_total]
    shared_part = segment[slot_total:]
    gate_routed = matmul(routed_part, gate_local)
    up_routed = matmul(routed_part, up_local)
    gate_shared = matmul(shared_part, shared_gate)
    up_shared = matmul(shared_part, shared_up)
    routed_hidden = (jax.nn.silu(gate_routed) * up_routed).astype(jnp.bfloat16)
    shared_hidden = (jax.nn.silu(gate_shared) * up_shared).astype(jnp.bfloat16)
    hidden_stack = jnp.concatenate([routed_hidden, shared_hidden], axis=0)
    segment = lax.all_gather(hidden_stack, "ctx", axis=1, tiled=True)
    routed_out = matmul(segment[:slot_total], down_local)
    shared_out = matmul(segment[slot_total:], shared_down)
    routed_bf = routed_out.astype(jnp.bfloat16)
    sendback = routed_bf.reshape(group_count, member_count, capacity * out_width)
    returned = lax.all_to_all(
        lax.all_to_all(sendback, "node", split_axis=0, concat_axis=0, tiled=True),
        "local",
        split_axis=1,
        concat_axis=1,
        tiled=True,
    )
    returned = returned.reshape(slot_total, out_width)
    pair_out = returned[pair_slot].reshape(tok_count, top_count, out_width).astype(jnp.float32)
    weighted = gate_weights[:, :, None] * pair_out
    group_sum = jnp.einsum(
        "tkg,tkd->tgd", group_onehot.astype(jnp.float32), weighted, precision=lax.Precision.HIGHEST
    )
    rounded = lax.optimization_barrier(group_sum.astype(jnp.bfloat16)).astype(jnp.float32)
    routed_sum = jnp.sum(rounded, axis=1)
    mixed = shared_out + routed_sum
    return mixed.astype(jnp.bfloat16)


def column_tiles(width, tile, visit):
    whole = width // tile
    if whole == 1:
        visit(0, tile)
    elif whole > 1:

        def step(index, carry):
            visit(pl.multiple_of(index * tile, tile), tile)
            return carry

        lax.fori_loop(0, whole, step, 0)
    if width % tile:
        visit(whole * tile, width % tile)


def cube_kernel(
    sizes,
    tok_in,
    ids_in,
    scores_in,
    wg_in,
    wu_in,
    wd_in,
    sg_in,
    su_in,
    sd_in,
    out_ref,
    tok,
    meta,
    wg,
    wu,
    wd,
    sg,
    su,
    sd,
    rows_in,
    hid_s,
    hid,
    part,
    got,
    total,
    sum_g,
    sum_u,
    hold,
    loc_sem,
    z_send,
    z_recv,
    b_send,
    b_recv,
    m_send,
    m_recv,
    p_send,
    p_recv,
):
    ctx_count, group_count, member_count, cap = sizes
    c = lax.axis_index("ctx")
    n = lax.axis_index("node")
    l = lax.axis_index("local")
    last = ctx_count - 1
    tok_count = tok.shape[2]
    feat = tok.shape[3]
    width = wg.shape[1]
    out_width = wd.shape[1]
    slots = range(1, tok.shape[0])

    def peer(slot):
        node = n
        if slot & 1:
            node = node + 1 - 2 * lax.rem(node, 2)
        if slot & 4:
            node = lax.rem(node + group_count // 2, group_count)
        member = lax.rem(l + 1, member_count) if slot & 2 else l
        return {"node": node, "local": member}

    first = pltpu.make_async_copy(tok_in, tok.at[0, c], loc_sem.at[0])
    first.start()

    barrier = pltpu.get_barrier_semaphore()
    for slot in slots:
        pl.semaphore_signal(barrier, inc=1, device_id=peer(slot), device_id_type=MESH)

    @pl.when(c > 0)
    def _():
        pl.semaphore_signal(barrier, inc=1, device_id={"ctx": c - 1}, device_id_type=MESH)

    @pl.when(c < last)
    def _():
        pl.semaphore_signal(barrier, inc=1, device_id={"ctx": c + 1}, device_id_type=MESH)

    loads = []
    for index, (src, dst) in enumerate(
        ((sg_in, sg), (su_in, su), (wg_in, wg), (wu_in, wu), (sd_in, sd), (wd_in, wd))
    ):
        loads.append(pltpu.make_async_copy(src, dst, loc_sem.at[2 + index]))

    inner = (c > 0) & (c < last)

    @pl.when(inner)
    def _():
        pl.semaphore_wait(barrier, len(slots) + 2)

    @pl.when(jnp.logical_not(inner))
    def _():
        pl.semaphore_wait(barrier, len(slots) + 1)

    first.wait()

    def piece(chunk, shard):
        if chunk == 0:
            return tok.at[0, shard]
        if chunk == 1:
            return hid_s.at[shard]
        return hid.at[chunk - 2, shard]

    def line(chunk, depth, way, shard, target):
        return pltpu.make_async_remote_copy(
            src_ref=piece(chunk, shard),
            dst_ref=piece(chunk, shard),
            send_sem=z_send.at[way, depth, chunk],
            recv_sem=z_recv.at[way, depth, chunk],
            device_id={"ctx": target},
            device_id_type=MESH,
        )

    def line_send(chunk, depth, finish=False):
        for way in (0, 1):
            shard, target = (c - depth, c + 1) if way == 0 else (c + depth, c - 1)
            ready = (c >= depth) & (c < last) if way == 0 else (c + depth <= last) & (c > 0)

            @pl.when(ready)
            def _():
                copy = line(chunk, depth, way, shard, target)
                if finish:
                    copy.wait_send()
                else:
                    copy.start()

    def line_take(chunk, depth, then=None):
        for way in (0, 1):
            shard = c - 1 - depth if way == 0 else c + 1 + depth
            ready = shard >= 0 if way == 0 else shard <= last

            @pl.when(ready)
            def _():
                source = c - 1 if way == 0 else c + 1
                line(chunk, depth, way, shard, source).wait_recv()
                target = c + 1 if way == 0 else c - 1
                if depth < last - 1:

                    @pl.when(target < ctx_count if way == 0 else target >= 0)
                    def _():
                        line(chunk, depth + 1, way, shard, target).start()

                if then is not None:
                    then(shard)

    def hand(src_slot, dst_slot, shard, over):
        return pltpu.make_async_remote_copy(
            src_ref=tok.at[src_slot, shard],
            dst_ref=tok.at[dst_slot, shard],
            send_sem=b_send.at[dst_slot, shard],
            recv_sem=b_recv.at[dst_slot, shard],
            device_id=peer(over),
            device_id_type=MESH,
        )

    def spread(shard):
        hand(0, 2, shard, 2).start()
        hand(0, 4, shard, 4).start()
        hand(0, 1, shard, 1).start()

    line_send(0, 0)
    spread(c)
    for load in loads:
        load.start()

    scores = scores_in[...]
    scaled = route_scale * scores / jnp.sum(scores, axis=0, keepdims=True)
    gates = scaled.astype(jnp.bfloat16).astype(jnp.float32)
    row = lax.broadcasted_iota(jnp.int32, meta.shape[1:], 0)
    named = jnp.zeros(row.shape, jnp.float32)
    table = jnp.zeros(row.shape, jnp.float32)
    for k in range(ids_in.shape[0]):
        expert = ids_in[k : k + 1, :]
        named = jnp.where(row == expert // member_count, 1.0, named)
        table = table + jnp.where(row == expert + group_count, gates[k : k + 1, :], 0.0)
    square = (tok_count, tok_count)
    before = lax.broadcasted_iota(jnp.int32, square, 0) < lax.broadcasted_iota(jnp.int32, square, 1)
    counts = matmul(named.astype(jnp.bfloat16), jnp.where(before, 1.0, 0.0).astype(jnp.bfloat16))
    meta[0] = jnp.where(row < group_count, jnp.where(named > 0.5, counts, -1.0), table)

    greet = []
    for slot in slots:
        greet.append(
            pltpu.make_async_remote_copy(
                src_ref=meta.at[0],
                dst_ref=meta.at[slot],
                send_sem=m_send.at[slot],
                recv_sem=m_recv.at[slot],
                device_id=peer(slot),
                device_id_type=MESH,
            )
        )
        greet[-1].start()

    def shared_add(shard, fresh=False):
        ins = pl.ds(pl.multiple_of(shard * feat, 128), feat)

        def visit(start, size):
            cols = pl.ds(start, size)
            g = matmul(tok[0, shard], sg[ins, cols])
            u = matmul(tok[0, shard], su[ins, cols])
            sum_g[:, cols] = g if fresh else sum_g[:, cols] + g
            sum_u[:, cols] = u if fresh else sum_u[:, cols] + u

        column_tiles(width, 256, visit)

    loads[0].wait()
    loads[1].wait()
    shared_add(c, True)
    for depth in range(last):
        line_take(0, depth, spread)
        for shard in (c - 1 - depth, c + 1 + depth):

            @pl.when((shard >= 0) & (shard <= last))
            def _():
                shared_add(shard)


    rank_of = lambda slot: meta[slot, pl.ds(n, 1), :]
    weight_of = lambda slot: meta[slot, pl.ds(group_count + n * member_count + l, 1), :]

    def pick(row, slot):
        spots = lax.broadcasted_iota(jnp.int32, (cap, tok_count), 0).astype(jnp.float32)
        mask = jnp.where(spots == rank_of(slot), 1.0, 0.0).astype(jnp.bfloat16)

        def step(shard, carry):
            chosen = matmul(mask, tok[slot, shard]).astype(jnp.bfloat16)
            rows_in[row : row + cap, pl.ds(pl.multiple_of(shard * feat, 128), feat)] = chosen
            return carry

        lax.fori_loop(0, ctx_count, step, 0)

    def hidden(count, gate, up, target):
        def visit(start, size):
            cols = pl.ds(start, size)
            g = matmul(rows_in[0:count, :], gate[:, cols])
            u = matmul(rows_in[0:count, :], up[:, cols])
            target[:, cols] = (g / (1.0 + jnp.exp(-g)) * u).astype(jnp.bfloat16)

        column_tiles(width, 256, visit)

    pairs = ((2, 3), (4, 5), (6, 7), (0, 1))

    def compute(index):
        for place, slot in enumerate(pairs[index]):
            pick(place * cap, slot)
        hidden(2 * cap, wg, wu, hid.at[index, c])

    half = ctx_count // 2

    def take(slot, shard):
        hand(0, slot, shard, 1).wait_recv()

    g = sum_g[...]
    hid_s[c] = (g / (1.0 + jnp.exp(-g)) * sum_u[...]).astype(jnp.bfloat16)
    line_send(1, 0)

    for copy in greet:
        copy.wait_recv()
    loads[2].wait()
    loads[3].wait()
    for shard in range(ctx_count):
        take(1, shard)
    compute(3)
    line_send(5, 0)
    line_take(1, 0)
    for shard in range(ctx_count):
        take(2, shard)
        hand(2, 3, shard, 1).start()
        if shard < half:
            hand(2, 6, shard, 4).start()
        take(4, shard)
        hand(4, 5, shard, 1).start()
        if shard >= half:
            hand(4, 6, shard, 2).start()
    for shard in range(ctx_count):
        take(3, shard)
    compute(0)
    line_send(2, 0)
    line_take(1, 1)
    for shard in range(ctx_count):
        take(5, shard)
    compute(1)
    line_send(3, 0)
    line_take(2, 0)
    line_take(1, 2)

    loads[4].wait()
    loads[5].wait()

    def product(chunk, down, cols):
        value = matmul(piece(chunk, 0)[...], down[0:width, cols])
        for shard in range(1, ctx_count):
            value = value + matmul(
                piece(chunk, shard)[...], down[shard * width : (shard + 1) * width, cols]
            )
        return value

    def shared_down(start, size):
        cols = pl.ds(start, size)
        total[:, cols] = product(1, sd, cols)

    column_tiles(out_width, 256, shared_down)

    sends = {}

    def ship(slot, over):
        sends[slot] = pltpu.make_async_remote_copy(
            src_ref=part.at[slot - 1],
            dst_ref=got.at[slot - 1],
            send_sem=p_send.at[slot],
            recv_sem=p_recv.at[slot],
            device_id=peer(over),
            device_id_type=MESH,
        )
        sends[slot].start()

    def finish(index):
        weights = []
        for slot in pairs[index]:
            spots = lax.broadcasted_iota(jnp.int32, (tok_count, tok_count), 0).astype(jnp.float32)
            mask = jnp.where(spots == rank_of(slot), weight_of(slot), 0.0)
            weights.append(jnp.transpose(mask)[:, 0:cap].astype(jnp.bfloat16))

        def visit(start, size):
            cols = pl.ds(start, size)
            rows = product(index + 2, wd, cols).astype(jnp.bfloat16)
            for place, slot in enumerate(pairs[index]):
                value = matmul(weights[place], rows[place * cap : (place + 1) * cap])
                if slot == 0:
                    total[:, cols] += value
                elif place == 0:
                    hold[:, cols] = value
                else:
                    part[slot - 1, :, cols] = value.astype(jnp.bfloat16)

        column_tiles(out_width, 256, visit)
        ship(pairs[index][1], 1)

    def forward(index):
        slot, other = pairs[index]
        sends[other].wait_recv()

        def visit(start, size):
            cols = pl.ds(start, size)
            value = hold[:, cols] + got[other - 1, :, cols].astype(jnp.float32)
            part[slot - 1, :, cols] = value.astype(jnp.bfloat16)

        column_tiles(out_width, 256, visit)
        ship(slot, slot)

    for shard in range(ctx_count):
        take(6, shard)
        hand(6, 7, shard, 1).start()
    line_take(2, 1)
    for shard in range(ctx_count):
        take(7, shard)
    compute(2)
    line_send(4, 0)
    line_take(3, 0)
    line_take(3, 1)
    line_take(2, 2)
    finish(0)
    line_take(4, 0)
    forward(0)
    line_take(4, 1)
    line_take(3, 2)
    finish(1)
    line_take(5, 0)
    forward(1)
    line_take(5, 1)
    line_take(4, 2)
    finish(2)
    forward(2)
    for slot in (2, 4):
        sends[slot].wait_recv()

    def gather_some(start, size):
        cols = pl.ds(start, size)
        value = total[:, cols]
        for slot in (2, 4):
            value = value + got[slot - 1, :, cols].astype(jnp.float32)
        total[:, cols] = value

    column_tiles(out_width, 256, gather_some)
    line_take(5, 2)
    finish(3)
    for slot in (6, 1):
        sends[slot].wait_recv()

    def gather_rest(start, size):
        cols = pl.ds(start, size)
        value = total[:, cols]
        for slot in (6, 1):
            value = value + got[slot - 1, :, cols].astype(jnp.float32)
        out_ref[:, cols] = value.astype(jnp.bfloat16)

    column_tiles(out_width, 256, gather_rest)

    for copy in list(sends.values()) + greet:
        copy.wait_send()
    for chunk in range(6):
        for depth in range(last):
            line_send(chunk, depth, finish=True)
    for shard in range(ctx_count):
        for slot in (1, 2, 3, 4, 5, 6, 7):
            hand(0, slot, shard, 1).wait_send()


def cube(
    tokens, expert_ids, route_scores, w_gate, w_up, w_down, shared_gate, shared_up, shared_down
):
    ctx_count = lax.axis_size("ctx")
    group_count = lax.axis_size("node")
    member_count = lax.axis_size("local")
    expert_count = group_count * member_count
    tok_count, feat = tokens.shape
    cap = (10 * tok_count + 4 * group_count - 1) // (4 * group_count)
    hidden_units, out_width = w_down.shape[1:]
    width = w_gate.shape[2]
    meta_rows = -(-(group_count + expert_count) // 16) * 16
    slots = 2 * group_count
    bf16 = jnp.bfloat16
    rows = max(2 * cap, tok_count)
    anywhere = pl.BlockSpec(memory_space=pl.ANY)
    inside = pl.BlockSpec(memory_space=pltpu.VMEM)
    dma = pltpu.SemaphoreType.DMA
    kernel = lambda *refs: cube_kernel((ctx_count, group_count, member_count, cap), *refs)
    return pl.pallas_call(
        kernel,
        out_shape=jax.ShapeDtypeStruct((tok_count, out_width), bf16),
        in_specs=[anywhere, inside, inside] + [anywhere] * 6,
        out_specs=inside,
        scratch_shapes=[
            pltpu.VMEM((slots, ctx_count, tok_count, feat), bf16),
            pltpu.VMEM((slots, meta_rows, tok_count), jnp.float32),
            pltpu.VMEM(w_gate.shape[1:], bf16),
            pltpu.VMEM(w_up.shape[1:], bf16),
            pltpu.VMEM(w_down.shape[1:], bf16),
            pltpu.VMEM(shared_gate.shape, bf16),
            pltpu.VMEM(shared_up.shape, bf16),
            pltpu.VMEM(shared_down.shape, bf16),
            pltpu.VMEM((rows, ctx_count * feat), bf16),
            pltpu.VMEM((ctx_count, tok_count, width), bf16),
            pltpu.VMEM((4, ctx_count, 2 * cap, width), bf16),
            pltpu.VMEM((slots - 1, tok_count, out_width), bf16),
            pltpu.VMEM((slots - 1, tok_count, out_width), bf16),
            pltpu.VMEM((tok_count, out_width), jnp.float32),
            pltpu.VMEM((tok_count, width), jnp.float32),
            pltpu.VMEM((tok_count, width), jnp.float32),
            pltpu.VMEM((tok_count, out_width), jnp.float32),
            dma((8,)),
            dma((2, ctx_count - 1, 6)),
            dma((2, ctx_count - 1, 6)),
            dma((slots, ctx_count)),
            dma((slots, ctx_count)),
            dma((slots,)),
            dma((slots,)),
            dma((slots,)),
            dma((slots,)),
        ],
        compiler_params=pltpu.CompilerParams(
            collective_id=0, has_side_effects=True, vmem_limit_bytes=VMEM_BYTES
        ),
    )(
        tokens,
        expert_ids.T,
        route_scores.T,
        w_gate[0],
        w_up[0],
        w_down[0],
        shared_gate,
        shared_up,
        shared_down,
    )


def local(tokens, expert_ids, *rest):
    whole_groups = expert_ids.shape[1] == 2 * lax.axis_size("local")
    if whole_groups and lax.axis_size("local") == 2 and lax.axis_size("node") == 4:
        return cube(tokens, expert_ids, *rest)
    return exchange(tokens, expert_ids, *rest)


def solution(mesh):
    return jax.shard_map(
        local,
        mesh=mesh,
        in_specs=(
            P(("node", "local"), "ctx"),
            P(("node", "local"), None),
            P(("node", "local"), None),
            P(("node", "local"), None, "ctx"),
            P(("node", "local"), None, "ctx"),
            P(("node", "local"), None, "ctx"),
            P(None, "ctx"),
            P(None, "ctx"),
            P(None, "ctx"),
        ),
        out_specs=P(("node", "local"), "ctx"),
        check_vma=False,
    )
```
